256 devices in a mesh: pair: 64 (over z, y, core), win: 4 (over x).
Axes of the slice: x: 4, y: 4, z: 8, core: 2. Of those that a mesh axis runs over, the one named last changes fastest.
Arguments:
- spectra: bfloat16 [64, 16, 2, 512, 256], P('pair', None, None, 'win'), may hold values from -6 to 6
- partners: int32 [64, 3], P('pair'), may hold values from -1 to 63, as said below
Outputs:
- stacks: bfloat16 [16, 64, 3, 256, 2, 256], P('win', 'pair')
The draws below stay inside these ranges and needn't reach their ends.
Inputs may be any that keep to these rules, and one draw needn't show every extreme that they name: `partners`: row a lists distinct partner blocks among a + 1 to a + 5 in its first slots, at most 3 of them; the remaining slots hold -1.
All inputs are finite; a program needn't handle non-finite values.
Results may differ from the reference program's by a relative error of at most 0.001.
Values may be sent and summed in bfloat16 or wider, within the bound.
No kernel may reach another device: no remote copies, remote signals or barrier semaphores. Data moves between devices by JAX's collectives and lax.ppermute only.
A program may use at most 128 MiB of HBM per device.

```python
import math
import jax
import jax.numpy as jnp
from jax import lax

BCH = 256
F = 16
REACH = 5
PMAX = 3
WINDOWS = 512
NBLK = 64


def draw_partners(key, part):
    first_key, second_key = jax.random.split(jax.random.fold_in(key, 17))
    blocks = jnp.arange(NBLK, dtype=jnp.int32)
    offsets = jnp.arange(1, REACH + 1, dtype=jnp.int32)
    levels = jax.random.randint(first_key, (NBLK,), 0, 10)
    wanted = jnp.where(levels < 7, 1, jnp.where(levels < 8, 2, 3)).astype(jnp.int32)
    wanted = jnp.minimum(wanted, PMAX)
    wanted = wanted.at[0].set(PMAX).at[1].set(PMAX)
    scores = jax.random.randint(second_key, (NBLK, REACH), 0, 4096).astype(jnp.int32) * 8 + offsets[None, :]
    scores = scores.at[0].set(REACH + 1 - offsets).at[1].set(offsets)
    beyond = blocks[:, None] + offsets[None, :] >= NBLK
    scores = jnp.where(beyond, scores + (1 << 20), scores)
    order = jnp.argsort(scores, axis=1, stable=True)
    chosen = jnp.take_along_axis(jnp.broadcast_to(offsets[None, :], (NBLK, REACH)), order[:, :PMAX], axis=1)
    available = jnp.clip(NBLK - 1 - blocks, 0, REACH)
    counted = jnp.minimum(wanted, available)
    slots = jnp.arange(PMAX, dtype=jnp.int32)
    return jnp.where(slots[None, :] < counted[:, None], blocks[:, None] + chosen, -1).astype(jnp.int32)


def block_scale(rng, extent, cuts, smallest, largest):
    gain = 1.0
    for position, blocks in cuts:
        heights = jax.random.uniform(jax.random.fold_in(jax.random.fold_in(rng, 6), position), (blocks,), jnp.float32, smallest / len(cuts), largest / len(cuts))
        gain = gain * jnp.repeat(jnp.exp(heights), extent[position] // blocks).reshape((-1,) + (1,) * (len(extent) - 1 - position))
    return gain


def normal_values(own_key, dims, spread, reach, pieces=(), kind=jnp.bfloat16):
    entries = jax.random.normal(own_key, dims, jnp.float32) * spread
    if len(pieces) > 0:
        entries = block_scale(own_key, dims, pieces, -0.22, 0.18) * entries
    return jnp.clip(entries, min=-reach, max=reach).astype(kind)


def setup_inputs(seed: int = 0) -> dict:
    arg_keys = jax.random.split(jax.random.key(seed), 3)
    spectra = normal_values(arg_keys[0], (NBLK, F, 2, WINDOWS, BCH), 1.0, 6.0, ((0, 64), (3, 4)))
    partners = draw_partners(jax.random.fold_in(arg_keys[2], 71), 0)
    return {"spectra": spectra, "partners": partners}


def cross_block(own_block, partner_block):
    freq_count, two_parts, window_count, channels = own_block.shape
    left = own_block.astype(jnp.float32).reshape(freq_count, two_parts * window_count, channels)
    partner_f = partner_block.astype(jnp.float32)
    right_real = partner_f.reshape(freq_count, two_parts * window_count, channels)
    right_imag = jnp.concatenate([partner_f[:, 1], -partner_f[:, 0]], axis=1)
    right = jnp.concatenate([right_real, right_imag], axis=2)
    product = jnp.einsum('fkc,fke->fce', left, right)
    return product.reshape(freq_count, channels, 2, channels)

def reference(spectra, partners):
    norm_scale = 1.0 / math.sqrt(2.0 * WINDOWS)

    def one_block(block_index):
        own_block = lax.dynamic_index_in_dim(spectra, block_index, 0, keepdims=False)
        results = []
        for slot_index in range(PMAX):
            partner = lax.dynamic_index_in_dim(partners, block_index, 0, keepdims=False)[slot_index]
            usable = partner >= 0
            partner_block = lax.dynamic_index_in_dim(spectra, jnp.maximum(partner, 0).astype(jnp.int32), 0, keepdims=False)
            value = cross_block(own_block, partner_block) * norm_scale
            results.append(jnp.where(usable, value, jnp.zeros_like(value)))
        return jnp.stack(results, 1).astype(jnp.bfloat16)
    mapped = lax.map(one_block, jnp.arange(NBLK, dtype=jnp.int32))
    return jnp.transpose(mapped, (1, 0, 2, 3, 4, 5))
```

```python
import math

import jax
import jax.numpy as jnp
from jax import lax
from jax.experimental import pallas as pl
from jax.experimental.pallas import tpu as pltpu
from jax.sharding import Mesh
from jax.sharding import PartitionSpec as P

SLOTS = 3
AXES = ("z", "y", "core", "win")


def send(value, sizes, move, keep=lambda z, y: True):
    nz, ny, nc, nw = sizes

    def index(z, y, q, w):
        return (((z % nz) * ny + y % ny) * nc + q % nc) * nw + w

    pairs = []
    for z in range(nz):
        for y in range(ny):
            if not keep(z, y):
                continue
            for q in range(nc):
                for w in range(nw):
                    pairs.append((index(z, y, q, w), index(*move(z, y, q), w)))
    return lax.ppermute(value, AXES, pairs)


def chip_back(ny):
    return lambda z, y, q: ((z, y - 1, q) if y > 0 else (z - 1, ny - 1, q))


def left_kernel(own, left, mix):
    channels = own.shape[-1]
    rows = lax.broadcasted_iota(jnp.int32, (2 * channels, channels), 0)
    cols = lax.broadcasted_iota(jnp.int32, (2 * channels, channels), 1)
    even = jnp.where(rows == 2 * cols, 1.0, 0.0).astype(jnp.bfloat16)
    odd = jnp.where(rows == 2 * cols + 1, 1.0, 0.0).astype(jnp.bfloat16)
    mix[:, :channels] = even
    mix[:, channels:] = odd
    wins = own.shape[1] * own.shape[3]
    for r in range(2):
        cos = own[r, :, 0].reshape(wins, channels)
        sin = own[r, :, 1].reshape(wins, channels)
        for part, joined in ((0, (cos, -sin)), (1, (sin, cos))):
            both = jnp.concatenate(joined, axis=1)
            got = lax.dot_general(
                mix[...], both, (((1,), (1,)), ((), ())), preferred_element_type=jnp.float32
            )
            left[r, :, part * wins : (part + 1) * wins] = got.astype(jnp.bfloat16)


def pair_kernel(scale, table, left, own, next1, next2a, next2b, next3, next3z, out, held, sems):
    side, slot = pl.program_id(0), pl.program_id(1)
    first = jnp.logical_and(side == 0, slot == 0)

    def copies():
        return [
            pltpu.make_async_copy(own, held.at[pl.ds(0, 2)], sems.at[0]),
            pltpu.make_async_copy(next1, held.at[pl.ds(2, 2)], sems.at[1]),
            pltpu.make_async_copy(next2a, held.at[4], sems.at[2]),
            pltpu.make_async_copy(next2b, held.at[5], sems.at[3]),
        ]

    @pl.when(first)
    def _():
        for copy in copies():
            copy.start()

        @pl.when(table[8] == 0)
        def _():
            pltpu.make_async_copy(next3, held.at[6], sems.at[4]).start()

        @pl.when(table[8] != 0)
        def _():
            pltpu.make_async_copy(next3z, held.at[6], sems.at[4]).start()

        for copy in copies():
            copy.wait()
        pltpu.make_async_copy(next3, held.at[6], sems.at[4]).wait()

    which = table[side * 3 + slot]
    channels = left.shape[1] // 2

    @pl.when(which < 0)
    def _():
        out[...] = jnp.zeros_like(out)

    @pl.when(which >= 0)
    def _():
        block = jnp.maximum(which, 0)
        right = jnp.concatenate(
            [held[block, :, part].reshape(left.shape[2] // 2, channels) for part in range(2)], axis=0
        )
        got = jnp.dot(left[0], right, preferred_element_type=jnp.float32) * scale
        out[0, 0] = got.astype(jnp.bfloat16)


def solution(mesh):
    nw = mesh.shape["win"]
    ny, nc = 4, 2
    nz = mesh.shape["pair"] // (ny * nc)
    sizes = (nz, ny, nc, nw)
    fine = Mesh(mesh.devices.reshape(sizes), AXES)

    def make_left(own):
        _, _, _, wins, channels = own.shape
        return pl.pallas_call(
            left_kernel,
            out_shape=jax.ShapeDtypeStruct((2, 2 * channels, 2 * nw * wins), jnp.bfloat16),
            scratch_shapes=[pltpu.VMEM((2 * channels, 2 * channels), jnp.bfloat16)],
            cost_estimate=pl.CostEstimate(flops=2**30, bytes_accessed=3 * 2**20, transcendentals=0),
            name="left",
        )(own)

    def pair_products(scale, table, left, own, *others):
        channels = own.shape[-1]
        return pl.pallas_call(
            lambda *refs: pair_kernel(scale, *refs),
            grid_spec=pltpu.PrefetchScalarGridSpec(
                num_scalar_prefetch=1,
                grid=(2, SLOTS),
                in_specs=[pl.BlockSpec((1, 2 * channels, left.shape[2]), lambda s, k, t: (t[6 + s], 0, 0))]
                + [pl.BlockSpec(memory_space=pl.ANY)] * (1 + len(others)),
                out_specs=pl.BlockSpec((1, 1, 2 * channels, channels), lambda s, k, t: (s, k, 0, 0)),
                scratch_shapes=[
                    pltpu.VMEM((7, *own.shape[1:]), jnp.bfloat16),
                    pltpu.SemaphoreType.DMA((5,)),
                ],
            ),
            out_shape=jax.ShapeDtypeStruct((2, SLOTS, 2 * channels, channels), jnp.bfloat16),
            cost_estimate=pl.CostEstimate(flops=2**31, bytes_accessed=6 * 2**20, transcendentals=0),
            name="pairs",
        )(table, left, own, *others)

    def local(spectra, partners):
        y, q = lax.axis_index("y"), lax.axis_index("core")
        z = lax.axis_index("z")
        freqs, parts, wins, channels = spectra.shape[1:]
        scale = 1.0 / math.sqrt(2.0 * wins * nw)
        per = freqs // (nw * nc)
        base = 2 * (z * ny + y)
        theirs = send(partners, sizes, lambda z, y, q: (z, y, 1 - q))
        rows = jnp.concatenate([theirs, partners], axis=0)
        picks = jnp.where(rows >= 0, jnp.clip(rows - base, 1, 6), -1).reshape(-1)
        table = jnp.concatenate([picks, jnp.stack([1 - q, q, jnp.where(y == 0, 0, 1)]).astype(jnp.int32)])
        grouped = spectra[0].reshape(nw, nc, per, parts, wins, channels)

        owns = []
        for j in range(per):
            piece = jnp.transpose(grouped[:, :, j], (1, 0, 2, 3, 4)).reshape(nc * nw, parts, wins, channels)
            got = lax.all_to_all(piece, ("core", "win"), 0, 0, tiled=True)
            owns.append(got.reshape(nc, nw, parts, wins, channels))

        kept, returned = [], []
        for j in range(per):
            own = owns[j]
            next1 = send(own, sizes, chip_back(ny))
            ahead = send(own[0], sizes, lambda z, y, q: (z, y + 1, q))
            ahead_z = send(ahead, sizes, lambda z, y, q: (z - 1, y, q), lambda z, y: y > 0)
            next2b = send(next1[1], sizes, chip_back(ny))
            relay = jnp.where(jnp.logical_or(y == 0, y == ny - 1), ahead, ahead_z)
            next2a = send(relay, sizes, lambda z, y, q: (z, y + 1, q))
            left = make_left(own)
            out = pair_products(scale, table, left, own, next1, next2a, next2b, ahead, ahead_z)
            kept.append(out[1])
            returned.append(send(out[0], sizes, lambda z, y, q: (z, y, 1 - q)))

        kept, returned = jnp.stack(kept), jnp.stack(returned)
        low, high = jnp.where(q == 0, kept, returned), jnp.where(q == 0, returned, kept)
        full = jnp.concatenate([low, high], axis=0)
        return full.reshape(nc * per, 1, SLOTS, channels, 2, channels)

    pair = ("z", "y", "core")
    return jax.shard_map(
        local,
        mesh=fine,
        in_specs=(P(pair, None, None, "win", None), P(pair, None)),
        out_specs=P("win", pair, None, None, None, None),
        check_vma=False,
    )
```
